32 devices in a mesh: dp: 16 (over z, y, core), pair: 2 (over x).
Axes of the slice: x: 2, y: 2, z: 4, core: 2. Of those that a mesh axis runs over, the one named last changes fastest.
Arguments:
- latents: bfloat16 [64, 256, 768], P(('dp', 'pair')), may hold values from -6 to 6
- conditioning: bfloat16 [64, 768], P(('dp', 'pair')), may hold values from -6 to 6
- cotangent: bfloat16 [64, 256, 768], P(('dp', 'pair')), may hold values from -6 to 6
- adaln_weight: bfloat16 [2, 768, 4608], P(None, ('dp', 'pair')), may hold values from -0.21875 to 0.21875
- adaln_bias: bfloat16 [2, 4608], P(None, ('dp', 'pair')), may hold values from -3 to 3
- qkv_weight: bfloat16 [2, 768, 2304], P(None, ('dp', 'pair')), may hold values from -0.21875 to 0.21875
- query_bias: bfloat16 [2, 768], P(None, ('dp', 'pair')), may hold values from -3 to 3
- value_bias: bfloat16 [2, 768], P(None, ('dp', 'pair')), may hold values from -3 to 3
- proj_weight: bfloat16 [2, 768, 768], P(None, ('dp', 'pair')), may hold values from -0.875 to 0.875
- proj_bias: bfloat16 [2, 768], P(None, ('dp', 'pair')), may hold values from -3 to 3
- expand_weight: bfloat16 [2, 768, 3072], P(None, ('dp', 'pair')), may hold values from -0.21875 to 0.21875
- expand_bias: bfloat16 [2, 3072], P(None, ('dp', 'pair')), may hold values from -3 to 3
- reduce_weight: bfloat16 [2, 3072, 768], P(None, ('dp', 'pair')), may hold values from -0.109375 to 0.109375
- reduce_bias: bfloat16 [2, 768], P(None, ('dp', 'pair')), may hold values from -3 to 3
Outputs:
- outputs: bfloat16 [64, 256, 768], P(('dp', 'pair'))
- grad_latents: float32 [64, 256, 768], P(('dp', 'pair'))
- grad_conditioning: float32 [64, 768], P(('dp', 'pair'))
- grad_adaln_weight: float32 [2, 768, 4608], P(None, ('dp', 'pair'))
- grad_adaln_bias: float32 [2, 4608], P(None, ('dp', 'pair'))
- grad_qkv_weight: float32 [2, 768, 2304], P(None, ('dp', 'pair'))
- grad_query_bias: float32 [2, 768], P(None, ('dp', 'pair'))
- grad_value_bias: float32 [2, 768], P(None, ('dp', 'pair'))
- grad_proj_weight: float32 [2, 768, 768], P(None, ('dp', 'pair'))
- grad_proj_bias: float32 [2, 768], P(None, ('dp', 'pair'))
- grad_expand_weight: float32 [2, 768, 3072], P(None, ('dp', 'pair'))
- grad_expand_bias: float32 [2, 3072], P(None, ('dp', 'pair'))
- grad_reduce_weight: float32 [2, 3072, 768], P(None, ('dp', 'pair'))
- grad_reduce_bias: float32 [2, 768], P(None, ('dp', 'pair'))
The draws below stay inside these ranges and needn't reach their ends.
All inputs are finite; a program needn't handle non-finite values.
Results may differ from the reference program's by a relative error of at most 0.025.
The reference program's roundings to bfloat16 on the way count: a program that leaves them out, or rounds other values in their place, can miss the bound.
Values may be sent and summed in bfloat16 or wider, within the bound.
A program may use at most 256 MiB of HBM per device.

```python
import math
import jax
import jax.numpy as jnp
from jax import lax

D = 768
HEADS = 12
HEAD = 64
FF = 3072
SEQ = 256
LAYERS = 2
LATENTS = 64


def spiked(drawn, stream_key, source, target, blocks, factor):
    def block_of(axis_at):
        return (jnp.arange(drawn.shape[axis_at]) // (drawn.shape[axis_at] // blocks)).reshape((-1,) + (1,) * (drawn.ndim - 1 - axis_at))

    one_side = jax.random.permutation(stream_key, blocks)[block_of(target)]
    other_side = (block_of(target) + blocks // 2) % blocks
    return jnp.where((block_of(source) == one_side) | (block_of(source) == other_side), factor * drawn, drawn)


def block_levels(stream_key, shape, shards, low, high):
    gain = 1.0
    for position, blocks in shards:
        heights = jax.random.uniform(jax.random.fold_in(jax.random.fold_in(stream_key, 6), position), (blocks,), jnp.float32, low / len(shards), high / len(shards))
        gain = gain * jnp.repeat(jnp.exp(heights), shape[position] // blocks).reshape((-1,) + (1,) * (len(shape) - 1 - position))
    return gain


def noise(key, extent, scale, limit, cuts=(), dtype=jnp.bfloat16):
    values = jax.random.normal(key, extent, jnp.float32) * scale
    if len(cuts) > 0:
        values = block_levels(key, extent, cuts, -0.22, 0.18) * values
    return jnp.clip(values, min=-limit, max=limit).astype(dtype)


def noise_with(rng, extent, deviation, reach, shards, heavy, held_as=jnp.bfloat16):
    array = deviation * jax.random.normal(rng, extent, jnp.float32)
    if shards:
        array = array * block_levels(rng, extent, shards, -0.22, 0.18)
    return jnp.clip(spiked(array, jax.random.fold_in(rng, 3), *heavy), -reach, reach).astype(held_as)


def setup_inputs(seed: int = 0) -> dict:
    seeds = jax.random.split(jax.random.key(seed), 15)
    return {
        "latents": noise(seeds[0], (LATENTS, SEQ, D), 1.0, 6.0, ((0, 32),)),
        "conditioning": noise(seeds[1], (LATENTS, D), 1.0, 6.0, ((0, 32),)),
        "cotangent": noise_with(seeds[2], (LATENTS, SEQ, D), 1.0, 6.0, ((0, 32),), (0, 2, 32, 2.75)),
        "adaln_weight": noise(seeds[3], (LAYERS, D, 6 * D), D ** -0.5, 0.21875, ((1, 32),)),
        "adaln_bias": noise(seeds[4], (LAYERS, 6 * D), 0.5, 3.0, ((1, 32),)),
        "qkv_weight": noise(seeds[5], (LAYERS, D, 3 * D), D ** -0.5, 0.21875, ((1, 32),)),
        "query_bias": noise(seeds[6], (LAYERS, D), 0.5, 3.0, ((1, 32),)),
        "value_bias": noise(seeds[7], (LAYERS, D), 0.5, 3.0, ((1, 32),)),
        "proj_weight": noise(seeds[8], (LAYERS, D, D), (D // 16) ** -0.5, 0.875, ((1, 32),)),
        "proj_bias": noise(seeds[9], (LAYERS, D), 0.5, 3.0, ((1, 32),)),
        "expand_weight": noise(seeds[10], (LAYERS, D, FF), D ** -0.5, 0.21875, ((1, 32),)),
        "expand_bias": noise(seeds[11], (LAYERS, FF), 0.5, 3.0, ((1, 32),)),
        "reduce_weight": noise(seeds[12], (LAYERS, FF, D), FF ** -0.5, 0.109375, ((1, 32),)),
        "reduce_bias": noise(seeds[13], (LAYERS, D), 0.5, 3.0, ((1, 32),)),
    }


PRECISE = lax.Precision.HIGHEST
EPSILON = 1e-06

@jax.custom_vjp
def low(v):
    return lax.optimization_barrier(v.astype(jnp.bfloat16)).astype(jnp.float32)

@jax.custom_vjp
def low_back(v):
    return v

def low_keep(v):
    return (low(v), None)

def low_pass(kept, grad):
    return (grad,)

def back_keep(v):
    return (v, None)

def back_low(kept, grad):
    return (low(grad),)
low.defvjp(low_keep, low_pass)
low_back.defvjp(back_keep, back_low)

def layer_norm(values):
    centre = values - lax.optimization_barrier(jnp.mean(values, axis=-1, keepdims=True))
    spread = lax.optimization_barrier(jnp.mean(centre * centre, axis=-1, keepdims=True))
    return centre * lax.rsqrt(spread + EPSILON)

def matmul(left, right):
    return jnp.dot(left, right, precision=PRECISE, preferred_element_type=jnp.float32)

def diffusion_transformer_block(residual_state, condition_vector, parameters):
    adaln_weight, adaln_bias, qkv_weight, query_bias, value_bias, proj_weight, proj_bias, expand_weight, expand_bias, reduce_weight, reduce_bias = parameters
    groups, length, width = residual_state.shape
    silu_low = low(jax.nn.silu(condition_vector))
    modulation = low_back(matmul(silu_low, adaln_weight) + adaln_bias)
    pieces = [piece[:, None, :] for piece in jnp.split(modulation, 6, axis=-1)]
    shift_attn, scale_attn, gate_attn, shift_mlp, scale_mlp, gate_mlp = pieces
    normed_in = low(layer_norm(residual_state) * (1.0 + scale_attn) + shift_attn)
    qkv_bias = jnp.concatenate([query_bias, jnp.zeros_like(query_bias), value_bias])
    qkv_rows = low(low_back(matmul(normed_in, qkv_weight) + qkv_bias))
    qkv_rows = qkv_rows.reshape(groups, length, 3, HEADS, HEAD)
    scores = low_back(jnp.einsum('gqhe,gkhe->ghqk', qkv_rows[:, :, 0], qkv_rows[:, :, 1], precision=PRECISE) * HEAD ** (-0.5))
    top_score = lax.optimization_barrier(jnp.max(scores, axis=-1, keepdims=True))
    weights_exp = jnp.exp(scores - top_score)
    probs = weights_exp / lax.optimization_barrier(jnp.sum(weights_exp, axis=-1, keepdims=True))
    attended = jnp.einsum('ghqk,gkhe->gqhe', low(probs), qkv_rows[:, :, 2], precision=PRECISE)
    attended = low(low_back(attended.reshape(groups, length, width)))
    attn_out = low_back(matmul(attended, proj_weight) + proj_bias)
    middle = residual_state + gate_attn * attn_out
    normed_mid = low(layer_norm(middle) * (1.0 + scale_mlp) + shift_mlp)
    pre_act = low_back(matmul(normed_mid, expand_weight) + expand_bias)
    activated = low(jax.nn.gelu(pre_act, approximate=True))
    mlp_out = low_back(matmul(activated, reduce_weight) + reduce_bias)
    return middle + gate_mlp * mlp_out

def group_forward(parameters, latent_group, condition_group):
    residual_state = latent_group
    for layer_number in range(LAYERS):
        residual_state = diffusion_transformer_block(residual_state, condition_group, tuple((weight_matrix[layer_number] for weight_matrix in parameters)))
    return residual_state

def whole_forward(latent_all, cond_all, parameters):
    group_size = math.gcd(LATENTS, max(1, 4096 // SEQ))
    group_count = LATENTS // group_size
    latent_groups = latent_all.reshape(group_count, group_size, SEQ, D)
    cond_groups = cond_all.reshape(group_count, group_size, D)
    checked = jax.checkpoint(group_forward)

    def step_fn(carry, inputs):
        return (carry, checked(parameters, inputs[0], inputs[1]))
    _, results = lax.scan(step_fn, jnp.int32(0), (latent_groups, cond_groups))
    return results.reshape(LATENTS, SEQ, D)

def reference(latents, conditioning, cotangent, adaln_weight, adaln_bias, qkv_weight, query_bias, value_bias, proj_weight, proj_bias, expand_weight, expand_bias, reduce_weight, reduce_bias):
    parameters = (adaln_weight.astype(jnp.float32), adaln_bias.astype(jnp.float32), qkv_weight.astype(jnp.float32), query_bias.astype(jnp.float32), value_bias.astype(jnp.float32), proj_weight.astype(jnp.float32), proj_bias.astype(jnp.float32), expand_weight.astype(jnp.float32), expand_bias.astype(jnp.float32), reduce_weight.astype(jnp.float32), reduce_bias.astype(jnp.float32))
    outputs, pull = jax.vjp(whole_forward, latents.astype(jnp.float32), conditioning.astype(jnp.float32), parameters)
    grad_latents, grad_conditioning, grads = pull(cotangent.astype(jnp.float32))
    return (outputs.astype(jnp.bfloat16), grad_latents, grad_conditioning, grads[0], grads[1], grads[2], grads[3], grads[4], grads[5], grads[6], grads[7], grads[8], grads[9], grads[10])
```

```python
import jax
import jax.numpy as jnp
from jax import lax
from jax.sharding import PartitionSpec as P

HEADS = 12
HEAD = 64
LAYERS = 2


EPSILON = 1e-06


def layer_norm(values):
    centre = values - jnp.mean(values, axis=-1, keepdims=True)
    spread = jnp.mean(centre * centre, axis=-1, keepdims=True)
    return centre * lax.rsqrt(spread + EPSILON)


def modulate(residual_state, shift, scale):
    return layer_norm(residual_state) * (1.0 + scale[:, None, :]) + shift[:, None, :]


def gelu_tanh(values):
    return jax.nn.gelu(values, approximate=True)


AXES = ("dp", "pair")
LANES = 128
GRAD_DTYPE = jnp.bfloat16


def pack_shards(shards, layer_number):
    (
        adaln_weight,
        adaln_bias,
        qkv_weight,
        query_bias,
        value_bias,
        proj_weight,
        proj_bias,
        expand_weight,
        expand_bias,
        reduce_weight,
        reduce_bias,
    ) = [member[layer_number] for member in shards]
    rows = qkv_weight.shape[0]
    pieces = reduce_weight.shape[0] // rows
    biases = jnp.concatenate(
        [adaln_bias, query_bias, value_bias, proj_bias, expand_bias, reduce_bias]
    )
    biases = jnp.pad(biases, (0, rows * LANES - biases.shape[0])).reshape(rows, LANES)
    reduce_parts = [reduce_weight[piece * rows : (piece + 1) * rows] for piece in range(pieces)]
    return jnp.concatenate(
        [adaln_weight, qkv_weight, proj_weight, expand_weight] + reduce_parts + [biases], axis=1
    )


def fetch(shards, layer_number, shard_count):
    block = pack_shards(shards, layer_number)
    rows = block.shape[0]
    full = lax.all_gather(block, AXES, axis=0, tiled=True)
    widths = [shards[0].shape[2], shards[2].shape[2], shards[5].shape[2], shards[7].shape[2]]
    weights = []
    at = 0
    for width in widths:
        weights.append(full[:, at : at + width])
        at += width
    reduce_cols = shards[9].shape[2]
    pieces = shards[9].shape[1] // rows
    reduce_weight = full[:, at : at + pieces * reduce_cols]
    reduce_weight = reduce_weight.reshape(shard_count, rows, pieces, reduce_cols)
    reduce_weight = reduce_weight.transpose(0, 2, 1, 3).reshape(-1, reduce_cols)
    at += pieces * reduce_cols
    flat = full[:, at:].reshape(shard_count, rows * LANES)
    biases = []
    at = 0
    for member in (1, 3, 4, 6, 8, 10):
        size = shards[member].shape[1]
        biases.append(flat[:, at : at + size].reshape(-1))
        at += size
    return (
        weights[0],
        biases[0],
        weights[1],
        biases[1],
        biases[2],
        weights[2],
        biases[3],
        weights[3],
        biases[4],
        reduce_weight,
        biases[5],
    )


def send_grads(totals, shard_count):
    (
        adaln_weight,
        adaln_bias,
        qkv_weight,
        query_bias,
        value_bias,
        proj_weight,
        proj_bias,
        expand_weight,
        expand_bias,
        reduce_weight,
        reduce_bias,
    ) = totals
    model_width = qkv_weight.shape[0]
    rows = model_width // shard_count
    reduce_cols = reduce_weight.shape[1]
    pieces = reduce_weight.shape[0] // model_width
    biases = [adaln_bias, query_bias, value_bias, proj_bias, expand_bias, reduce_bias]
    flat = jnp.concatenate([member.reshape(shard_count, -1) for member in biases], axis=1)
    bias_sizes = [member.shape[0] // shard_count for member in biases]
    flat = jnp.pad(flat, ((0, 0), (0, rows * LANES - flat.shape[1])))
    flat = flat.astype(GRAD_DTYPE).reshape(model_width, LANES)
    split = reduce_weight.astype(GRAD_DTYPE).reshape(shard_count, pieces, rows, reduce_cols)
    split = split.transpose(0, 2, 1, 3).reshape(model_width, pieces * reduce_cols)
    weights = [adaln_weight, qkv_weight, proj_weight, expand_weight]
    block = jnp.concatenate(
        [member.astype(GRAD_DTYPE) for member in weights] + [split, flat], axis=1
    )
    mine = lax.psum_scatter(block, AXES, scatter_dimension=0, tiled=True).astype(jnp.float32)
    out = []
    at = 0
    for member in weights:
        out.append(mine[:, at : at + member.shape[1]])
        at += member.shape[1]
    reduced = jnp.concatenate(
        [
            mine[:, at + piece * reduce_cols : at + (piece + 1) * reduce_cols]
            for piece in range(pieces)
        ],
        axis=0,
    )
    at += pieces * reduce_cols
    flat = mine[:, at:].reshape(-1)
    small = []
    at = 0
    for size in bias_sizes:
        small.append(flat[at : at + size])
        at += size
    return (
        out[0],
        small[0],
        out[1],
        small[1],
        small[2],
        out[2],
        small[3],
        out[3],
        small[4],
        reduced,
        small[5],
    )


def forward_layer(residual_state, cond_part, gathered):
    (
        adaln_weight,
        adaln_bias,
        qkv_weight,
        query_bias,
        value_bias,
        proj_weight,
        proj_bias,
        expand_weight,
        expand_bias,
        reduce_weight,
        reduce_bias,
    ) = gathered
    latent_count, seq_len, model_width = residual_state.shape
    inv_root = HEAD ** (-0.5)
    silu_low = jax.nn.silu(cond_part).astype(jnp.bfloat16)
    modulation = jnp.dot(
        silu_low, adaln_weight, preferred_element_type=jnp.float32
    ) + adaln_bias.astype(jnp.float32)
    shift_attn, scale_attn, gate_attn, shift_mlp, scale_mlp, gate_mlp = jnp.split(
        modulation, 6, axis=-1
    )
    normed_in = modulate(residual_state, shift_attn, scale_attn).astype(jnp.bfloat16)
    qkv_bias = jnp.concatenate([query_bias, jnp.zeros_like(query_bias), value_bias]).astype(
        jnp.float32
    )
    qkv_rows = (
        jnp.dot(normed_in, qkv_weight, preferred_element_type=jnp.float32) + qkv_bias
    ).astype(jnp.bfloat16)
    qkv_rows = qkv_rows.reshape(latent_count, seq_len, 3, HEADS, HEAD)
    scores = (
        jnp.einsum(
            "bqhe,bkhe->bhqk",
            qkv_rows[:, :, 0],
            qkv_rows[:, :, 1],
            preferred_element_type=jnp.float32,
        )
        * inv_root
    )
    top_score = jnp.max(scores, axis=-1, keepdims=True)
    weights_exp = jnp.exp(scores - top_score)
    total_exp = jnp.sum(weights_exp, axis=-1, keepdims=True)
    probs = weights_exp / total_exp
    log_total = top_score + jnp.log(total_exp)
    attended = jnp.einsum(
        "bhqk,bkhe->bqhe",
        probs.astype(jnp.bfloat16),
        qkv_rows[:, :, 2],
        preferred_element_type=jnp.float32,
    )
    attended = attended.astype(jnp.bfloat16).reshape(latent_count, seq_len, model_width)
    attn_out = jnp.dot(
        attended, proj_weight, preferred_element_type=jnp.float32
    ) + proj_bias.astype(jnp.float32)
    middle = residual_state + gate_attn[:, None, :] * attn_out
    normed_mid = modulate(middle, shift_mlp, scale_mlp).astype(jnp.bfloat16)
    pre_act = jnp.dot(
        normed_mid, expand_weight, preferred_element_type=jnp.float32
    ) + expand_bias.astype(jnp.float32)
    activated = gelu_tanh(pre_act).astype(jnp.bfloat16)
    mlp_out = jnp.dot(
        activated, reduce_weight, preferred_element_type=jnp.float32
    ) + reduce_bias.astype(jnp.float32)
    result = middle + gate_mlp[:, None, :] * mlp_out
    stored = (
        residual_state,
        silu_low,
        modulation,
        normed_in,
        qkv_rows,
        log_total,
        attended,
        attn_out,
        middle,
        normed_mid,
        pre_act,
        activated,
        mlp_out,
    )
    return (result, stored)


def backward_layer(upstream, cond_part, gathered, stored):
    (
        adaln_weight,
        adaln_bias,
        qkv_weight,
        query_bias,
        value_bias,
        proj_weight,
        proj_bias,
        expand_weight,
        expand_bias,
        reduce_weight,
        reduce_bias,
    ) = gathered
    (
        residual_state,
        silu_low,
        modulation,
        normed_in,
        qkv_rows,
        log_total,
        attended,
        attn_out,
        middle,
        normed_mid,
        pre_act,
        activated,
        mlp_out,
    ) = stored
    latent_count, seq_len, model_width = residual_state.shape
    inv_root = HEAD ** (-0.5)
    shift_attn, scale_attn, gate_attn, shift_mlp, scale_mlp, gate_mlp = jnp.split(
        modulation, 6, axis=-1
    )
    d_mlp = (gate_mlp[:, None, :] * upstream).astype(jnp.bfloat16)
    d_gate_mlp = jnp.sum(upstream * mlp_out, axis=1)
    g_reduce_w = jnp.einsum("bsf,bsd->fd", activated, d_mlp, preferred_element_type=jnp.float32)
    g_reduce_b = jnp.sum(d_mlp, axis=(0, 1), dtype=jnp.float32)
    d_act = jnp.einsum("bsd,fd->bsf", d_mlp, reduce_weight, preferred_element_type=jnp.float32)
    _, pull_gelu = jax.vjp(gelu_tanh, pre_act)
    d_pre = pull_gelu(d_act)[0].astype(jnp.bfloat16)
    g_expand_w = jnp.einsum("bsd,bsf->df", normed_mid, d_pre, preferred_element_type=jnp.float32)
    g_expand_b = jnp.sum(d_pre, axis=(0, 1), dtype=jnp.float32)
    d_normed_mid = jnp.einsum(
        "bsf,df->bsd", d_pre, expand_weight, preferred_element_type=jnp.float32
    )
    _, pull_mid = jax.vjp(modulate, middle, shift_mlp, scale_mlp)
    d_middle, d_shift_mlp, d_scale_mlp = pull_mid(d_normed_mid)
    d_middle = d_middle + upstream
    d_attn = (gate_attn[:, None, :] * d_middle).astype(jnp.bfloat16)
    d_gate_attn = jnp.sum(d_middle * attn_out, axis=1)
    g_proj_w = jnp.einsum("bsd,bse->de", attended, d_attn, preferred_element_type=jnp.float32)
    g_proj_b = jnp.sum(d_attn, axis=(0, 1), dtype=jnp.float32)
    d_attended = jnp.einsum("bse,de->bsd", d_attn, proj_weight, preferred_element_type=jnp.float32)
    d_attended = d_attended.astype(jnp.bfloat16).reshape(latent_count, seq_len, HEADS, HEAD)
    queries = qkv_rows[:, :, 0]
    key_rows = qkv_rows[:, :, 1]
    value_rows = qkv_rows[:, :, 2]
    scores = (
        jnp.einsum("bqhe,bkhe->bhqk", queries, key_rows, preferred_element_type=jnp.float32)
        * inv_root
    )
    probs = jnp.exp(scores - log_total)
    d_probs = jnp.einsum(
        "bqhe,bkhe->bhqk", d_attended, value_rows, preferred_element_type=jnp.float32
    )
    d_scores = (probs * (d_probs - jnp.sum(probs * d_probs, axis=-1, keepdims=True))).astype(
        jnp.bfloat16
    )
    d_values = jnp.einsum(
        "bhqk,bqhe->bkhe",
        probs.astype(jnp.bfloat16),
        d_attended,
        preferred_element_type=jnp.float32,
    )
    d_queries = (
        jnp.einsum("bhqk,bkhe->bqhe", d_scores, key_rows, preferred_element_type=jnp.float32)
        * inv_root
    )
    d_keys = (
        jnp.einsum("bhqk,bqhe->bkhe", d_scores, queries, preferred_element_type=jnp.float32)
        * inv_root
    )
    d_qkv = jnp.stack([d_queries, d_keys, d_values], axis=2).astype(jnp.bfloat16)
    d_qkv = d_qkv.reshape(latent_count, seq_len, 3 * model_width)
    g_qkv_w = jnp.einsum("bsd,bsf->df", normed_in, d_qkv, preferred_element_type=jnp.float32)
    g_query_b = jnp.sum(d_qkv[:, :, :model_width], axis=(0, 1), dtype=jnp.float32)
    g_value_b = jnp.sum(d_qkv[:, :, 2 * model_width :], axis=(0, 1), dtype=jnp.float32)
    d_normed_in = jnp.einsum("bsf,df->bsd", d_qkv, qkv_weight, preferred_element_type=jnp.float32)
    _, pull_in = jax.vjp(modulate, residual_state, shift_attn, scale_attn)
    d_stream, d_shift_attn, d_scale_attn = pull_in(d_normed_in)
    d_stream = d_stream + d_middle
    d_modulation = jnp.concatenate(
        [d_shift_attn, d_scale_attn, d_gate_attn, d_shift_mlp, d_scale_mlp, d_gate_mlp], axis=-1
    ).astype(jnp.bfloat16)
    g_adaln_w = jnp.einsum("bd,bf->df", silu_low, d_modulation, preferred_element_type=jnp.float32)
    g_adaln_b = jnp.sum(d_modulation, axis=0, dtype=jnp.float32)
    d_silu = jnp.einsum("bf,df->bd", d_modulation, adaln_weight, preferred_element_type=jnp.float32)
    _, pull_silu = jax.vjp(jax.nn.silu, cond_part)
    d_cond = pull_silu(d_silu)[0]
    grads = (
        g_adaln_w,
        g_adaln_b,
        g_qkv_w,
        g_query_b,
        g_value_b,
        g_proj_w,
        g_proj_b,
        g_expand_w,
        g_expand_b,
        g_reduce_w,
        g_reduce_b,
    )
    return (d_stream, d_cond, grads)


def on_device(
    latents,
    conditioning,
    cotangent,
    adaln_weight,
    adaln_bias,
    qkv_weight,
    query_bias,
    value_bias,
    proj_weight,
    proj_bias,
    expand_weight,
    expand_bias,
    reduce_weight,
    reduce_bias,
):
    shards = (
        adaln_weight,
        adaln_bias,
        qkv_weight,
        query_bias,
        value_bias,
        proj_weight,
        proj_bias,
        expand_weight,
        expand_bias,
        reduce_weight,
        reduce_bias,
    )
    shard_count = lax.axis_size(AXES)
    stream = latents.astype(jnp.float32)
    cond_part = conditioning.astype(jnp.float32)
    gathered = [fetch(shards, layer_number, shard_count) for layer_number in range(LAYERS)]
    stored = [None] * LAYERS
    for layer_number in range(LAYERS):
        stream, stored[layer_number] = forward_layer(stream, cond_part, gathered[layer_number])
    outputs = stream.astype(jnp.bfloat16)
    upstream = cotangent.astype(jnp.float32)
    grad_conditioning = jnp.zeros_like(cond_part)
    summed = [None] * LAYERS
    for layer_number in reversed(range(LAYERS)):
        upstream, cond_term, grads = backward_layer(
            upstream, cond_part, gathered[layer_number], stored[layer_number]
        )
        grad_conditioning = grad_conditioning + cond_term
        summed[layer_number] = send_grads(grads, shard_count)
    stacked = [
        jnp.stack([summed[layer_number][member] for layer_number in range(LAYERS)])
        for member in range(11)
    ]
    return tuple([outputs, upstream, grad_conditioning] + stacked)


def solution(mesh):
    in_specs = (
        P(("dp", "pair"), None, None),
        P(("dp", "pair"), None),
        P(("dp", "pair"), None, None),
        P(None, ("dp", "pair"), None),
        P(None, ("dp", "pair")),
        P(None, ("dp", "pair"), None),
        P(None, ("dp", "pair")),
        P(None, ("dp", "pair")),
        P(None, ("dp", "pair"), None),
        P(None, ("dp", "pair")),
        P(None, ("dp", "pair"), None),
        P(None, ("dp", "pair")),
        P(None, ("dp", "pair"), None),
        P(None, ("dp", "pair")),
    )
    out_specs = (
        P(("dp", "pair"), None, None),
        P(("dp", "pair"), None, None),
        P(("dp", "pair"), None),
        P(None, ("dp", "pair"), None),
        P(None, ("dp", "pair")),
        P(None, ("dp", "pair"), None),
        P(None, ("dp", "pair")),
        P(None, ("dp", "pair")),
        P(None, ("dp", "pair"), None),
        P(None, ("dp", "pair")),
        P(None, ("dp", "pair"), None),
        P(None, ("dp", "pair")),
        P(None, ("dp", "pair"), None),
        P(None, ("dp", "pair")),
    )
    return jax.shard_map(
        on_device, mesh=mesh, in_specs=in_specs, out_specs=out_specs, check_vma=False
    )
```
